32 devices in a mesh: ty: 8 (over z, x), tx: 4 (over y, core).
Axes of the slice: x: 2, y: 2, z: 4, core: 2. Of those that a mesh axis runs over, the one named last changes fastest.
Arguments:
- specimen: float32 [2, 2048, 4096], P(None, 'ty', 'tx'), may hold values from -5 to 5
- probe_modes: float32 [4, 2, 128, 128], replicated, may hold values from -0.75 to 0.75
- patterns: float32 [256, 128, 128], P(('ty', 'tx')), may hold values from 0.25 to 2.5
- tile_row: int32 [256], P(('ty', 'tx')), may hold values from 0 to 7, as said below
- row_offset: int32 [256], P(('ty', 'tx')), may hold values from 0 to 128
- col_offset: int32 [256], P(('ty', 'tx')), may hold values from 0 to 896
Outputs:
- specimen_out: float32 [2, 2048, 4096], P(None, 'ty', 'tx')
- probe_out: float32 [4, 2, 128, 128], replicated
The draws below stay inside these ranges and needn't reach their ends.
Inputs may be any that keep to these rules, and one draw needn't show every extreme that they name: `tile_row`: each index of ty+tx holds 8 consecutive positions. At most 2 of one device's positions name the same tile row, and for every index of tx some tile row is named exactly 2 times by each device with that tx index.
All inputs are finite; a program needn't handle non-finite values.
Results may differ from the reference program's by a relative error of at most 0.0001.
Values sent between devices are 32-bit elements; how exact they have to be, the bound alone decides.
A program may use at most 192 MiB of HBM per device.

```python
import math
import jax
import jax.numpy as jnp
from jax import lax

PATCH = 128
MODES = 4
TR = 256
TC = 1024
P_DEV = 8
ITERS = 2
GRID_ROWS = 8
GRID_COLS = 4
CAP = 2
NPOS = 256
OBJ_R = 2048
OBJ_C = 4096


def draw_tile_row(key, part):
    devices_all = GRID_ROWS * GRID_COLS
    slot_total = GRID_ROWS * CAP
    key_hot = jax.random.fold_in(key, 11)
    key_pref = jax.random.fold_in(key, 23)
    key_jitter = jax.random.fold_in(key, 37)
    key_order = jax.random.fold_in(key, 41)
    hot_rows = jax.random.randint(key_hot, (GRID_COLS,), 0, GRID_ROWS)
    preferences = jax.random.randint(key_pref, (GRID_COLS, GRID_ROWS), 0, 4)
    jitter_values = jax.random.randint(key_jitter, (devices_all, slot_total), 0, 4096)
    device_ids = jnp.arange(devices_all, dtype=jnp.int32)
    column_ids = device_ids % GRID_COLS
    slot_ids = jnp.arange(slot_total, dtype=jnp.int32)
    slot_rows = slot_ids // CAP
    pref_table = preferences[column_ids][:, slot_rows]
    scores = (pref_table * 4096 + jitter_values) * 256 + slot_ids[None, :]
    is_hot = slot_rows[None, :] == hot_rows[column_ids][:, None]
    scores = jnp.where(is_hot, 16777216 + slot_ids[None, :], scores)
    chosen = lax.top_k(scores, P_DEV)[1]
    chosen_rows = (chosen // CAP).astype(jnp.int32)
    order_keys = jax.random.randint(key_order, (devices_all, P_DEV), 0, 4096) * 64 + jnp.arange(P_DEV, dtype=jnp.int32)[None, :]
    ordering = jnp.argsort(order_keys, axis=1)
    shuffled = jnp.take_along_axis(chosen_rows, ordering, axis=1)
    return shuffled.reshape(-1).astype(jnp.int32)


def draw_probe_modes(key, part):
    key_amp = jax.random.fold_in(key, 5)
    key_phase = jax.random.fold_in(key, 7)
    lower_end = 0.8
    radius_frac = 0.42
    floor_level = 0.25
    counter = jnp.arange(PATCH, dtype=jnp.float32) - (PATCH - 1) / 2.0
    rho_sq = (counter[:, None] ** 2 + counter[None, :] ** 2) / (radius_frac * PATCH) ** 2
    envelope = floor_level + (1.0 - floor_level) * jnp.exp(-rho_sq ** 4)
    mode_weight = 0.75 * 0.68 ** jnp.arange(MODES, dtype=jnp.float32)
    amplitude = jax.random.uniform(key_amp, (MODES, PATCH, PATCH), jnp.float32, lower_end, 1.0)
    phases = jax.random.uniform(key_phase, (MODES, PATCH, PATCH), jnp.float32, -math.pi, math.pi)
    magnitude = mode_weight[:, None, None] * amplitude * envelope[None]
    return jnp.stack([magnitude * jnp.cos(phases), magnitude * jnp.sin(phases)], axis=1).astype(jnp.float32)


def place_ends(result, key, low, top_value):
    longest = result.shape.index(max(result.shape))
    spots = []
    for shift in (0, 1):
        where = [jax.random.randint(jax.random.fold_in(key, axis), (), 0, length) for axis, length in enumerate(result.shape)]
        where[longest] = (where[longest] + shift) % result.shape[longest]
        spots.append(tuple(where))
    return result.at[spots[0]].set(low).at[spots[1]].set(top_value)


def shard_levels(stream_key, dims, cuts, smallest, top_value):
    gain, own = 1.0, jax.random.fold_in(stream_key, 6)
    for dim, shards_of in cuts:
        steps = jnp.exp(jax.random.uniform(jax.random.fold_in(own, dim), (shards_of,), jnp.float32, smallest / len(cuts), top_value / len(cuts)))
        gain = gain * jnp.repeat(steps, dims[dim] // shards_of).reshape([-1 if axis == dim else 1 for axis in range(len(dims))])
    return gain


def gaussian(key, shape, deviation, most, split=(), kind=jnp.bfloat16):
    factor_of = shard_levels(key, shape, split, -0.22, 0.18) if split else 1.0
    array = jax.random.normal(key, shape, jnp.float32) * deviation * factor_of
    return jnp.minimum(jnp.maximum(array, -most), most).astype(kind)


def setup_inputs(seed: int = 0) -> dict:
    arg_keys = jax.random.split(jax.random.key(seed), 7)
    return {
        "specimen": gaussian(arg_keys[0], (2, OBJ_R, OBJ_C), 0.7, 5.0, ((1, 8), (2, 4)), jnp.float32),
        "probe_modes": draw_probe_modes(jax.random.fold_in(arg_keys[6], 71), 0),
        "patterns": jnp.clip(0.25 + 2.25 * jax.random.uniform(arg_keys[2], (NPOS, PATCH, PATCH), jnp.float32) ** shard_levels(arg_keys[2], (NPOS, PATCH, PATCH), ((0, 32),), -0.2, 0.2), 0.25, 2.5),
        "tile_row": draw_tile_row(jax.random.fold_in(arg_keys[6], 71), 0),
        "row_offset": place_ends(jax.random.randint(arg_keys[4], (NPOS,), 0, TR - PATCH + 1), jax.random.fold_in(arg_keys[4], 1), 0, TR - PATCH).astype(jnp.int32),
        "col_offset": place_ends(jax.random.randint(arg_keys[5], (NPOS,), 0, TC - PATCH + 1), jax.random.fold_in(arg_keys[5], 1), 0, TC - PATCH).astype(jnp.int32),
    }


AMP_FLOOR = 0.3
OBJ_STEP = 1.0
SMALL_EPS = 1e-06

def position_terms(window_cut, probe_modes, intensity):
    window_c = window_cut[0] + 1j * window_cut[1]
    modes_c = probe_modes[:, 0] + 1j * probe_modes[:, 1]
    exit_wave = modes_c * window_c[None]
    far_field = jnp.fft.fft2(exit_wave, norm='ortho')
    model_power = lax.optimization_barrier(jnp.sum(jnp.real(far_field) ** 2 + jnp.imag(far_field) ** 2, axis=0))
    factor = jnp.sqrt(intensity) / jnp.maximum(jnp.sqrt(model_power), AMP_FLOOR) - 1.0
    change = jnp.fft.ifft2(far_field * factor[None], norm='ortho')
    grad_window = lax.optimization_barrier(jnp.sum(jnp.conj(modes_c) * change, axis=0))
    grad_modes = jnp.conj(window_c)[None] * change
    lighting = window_cut[0] ** 2 + window_cut[1] ** 2
    return (jnp.stack([jnp.real(grad_window), jnp.imag(grad_window)]), jnp.stack([jnp.real(grad_modes), jnp.imag(grad_modes)], axis=1), lighting)

def reference(specimen, probe_modes, patterns, tile_row, row_offset, col_offset):
    index_all = jnp.arange(NPOS, dtype=jnp.int32)
    band_index = index_all // P_DEV % GRID_COLS
    rows_at = (tile_row * TR + row_offset).astype(jnp.int32)
    cols_at = (band_index * TC + col_offset).astype(jnp.int32)
    anchor = jnp.int32(0)
    for sweep_index in range(ITERS):
        current = specimen

        def visit_one(running, inputs):
            grad_sum, light_sum = running
            row_at, col_at, intensity = inputs
            window_cut = lax.dynamic_slice(current, (anchor, row_at, col_at), (2, PATCH, PATCH))
            grad_window, grad_modes, lighting = position_terms(window_cut, probe_modes, intensity)
            return ((grad_sum + grad_modes, light_sum + lighting), grad_window)
        initial = (jnp.zeros((MODES, 2, PATCH, PATCH), jnp.float32), jnp.zeros((PATCH, PATCH), jnp.float32))
        (grad_sum, light_sum), grad_windows = lax.scan(visit_one, initial, (rows_at, cols_at, patterns))
        probe_power = lax.optimization_barrier(jnp.sum(probe_modes[:, 0] ** 2 + probe_modes[:, 1] ** 2, axis=0))
        obj_scale = OBJ_STEP / (jnp.max(probe_power) + SMALL_EPS)

        def deposit(position, running_field):
            row_at = rows_at[position]
            col_at = cols_at[position]
            region = lax.dynamic_slice(running_field, (anchor, row_at, col_at), (2, PATCH, PATCH))
            return lax.dynamic_update_slice(running_field, region + obj_scale * grad_windows[position], (anchor, row_at, col_at))
        specimen = lax.fori_loop(0, NPOS, deposit, current)
        probe_modes = probe_modes + grad_sum / (jnp.max(light_sum) + SMALL_EPS)
    return (specimen, probe_modes)
```

```python
import functools
import math

import jax
import jax.numpy as jnp
import ml_dtypes
import numpy as np
from jax import lax
from jax.experimental import pallas as pl
from jax.experimental.pallas import tpu as pltpu
from jax.sharding import PartitionSpec as P

ITERS = 2
AMP_FLOOR = 0.3
OBJ_STEP = 1.0
SMALL_EPS = 1e-06

VMEM = pltpu.VMEM
SMEM = pltpu.SMEM
LIMIT = 50 * 1024 * 1024


def dft_tables(length):
    counter = np.arange(length, dtype=np.int64)
    angles = (counter[:, None] * counter[None, :] % length) * (2.0 * math.pi / length)
    cos = np.cos(angles) / math.sqrt(length)
    sin = np.sin(angles) / math.sqrt(length)
    one = np.block([[cos, sin], [-sin, cos]])
    parts = []
    for table in (one, one.T):
        high = table.astype(ml_dtypes.bfloat16)
        low = (table - high.astype(np.float64)).astype(ml_dtypes.bfloat16)
        parts += [high, low]
    return np.stack(parts)


def split(values):
    high = values.astype(jnp.bfloat16)
    low = (values - high.astype(jnp.float32)).astype(jnp.bfloat16)
    return high, low


def dot(a, b):
    return jnp.dot(a, b, preferred_element_type=jnp.float32)


def left(high, low, values):
    v_high, v_low = split(values)
    return dot(high, v_high) + (dot(low, v_high) + dot(high, v_low))


def right(values, high, low):
    v_high, v_low = split(values)
    return dot(v_high, high) + (dot(v_low, high) + dot(v_high, low))


def bucket_kernel(capacity, tile_ref, row_ref, col_ref, patterns_ref, grid_ref, req_ref):
    own = patterns_ref.shape[0]

    def clear(j, carry):
        req_ref[j] = 0
        return carry

    lax.fori_loop(0, req_ref.shape[0], clear, 0)
    for p in range(own):
        tile = tile_ref[p]
        rank = jnp.int32(0)
        for q in range(p):
            rank = rank + (tile_ref[q] == tile).astype(jnp.int32)
        slot = tile * capacity + rank
        grid_ref[slot] = patterns_ref[p]
        req_ref[slot * 3] = row_ref[p]
        req_ref[slot * 3 + 1] = col_ref[p]
        req_ref[slot * 3 + 2] = jnp.int32(1)


def bucket(tile_row, row_offset, col_offset, patterns, slots, capacity):
    window = patterns.shape[-1]
    return pl.pallas_call(
        functools.partial(bucket_kernel, capacity),
        out_shape=(
            jax.ShapeDtypeStruct((slots, window, window), jnp.float32),
            jax.ShapeDtypeStruct((slots * 3,), jnp.int32),
        ),
        in_specs=[pl.BlockSpec(memory_space=SMEM)] * 3 + [pl.BlockSpec(memory_space=VMEM)],
        out_specs=(pl.BlockSpec(memory_space=VMEM), pl.BlockSpec(memory_space=SMEM)),
        name="bucket",
    )(tile_row, row_offset, col_offset, patterns)


def sweep_kernel(req_ref, spec_ref, probe_ref, table_ref, pattern_ref, out_ref, grad_ref, scale_ref, far_ref):
    step = pl.program_id(0)
    modes, _, window, _ = probe_ref.shape
    tiles = window // 8

    @pl.when(step == 0)
    def _():
        out_ref[...] = spec_ref[...]
        grad_ref[...] = jnp.zeros_like(grad_ref)
        power = jnp.zeros((window, window), jnp.float32)
        for m in range(modes):
            power = power + (probe_ref[m, 0] ** 2 + probe_ref[m, 1] ** 2)
        scale_ref[0] = OBJ_STEP / (jnp.max(power) + SMALL_EPS)

    @pl.when(req_ref[step * 3 + 2] > 0)
    def _():
        row = req_ref[step * 3]
        col = req_ref[step * 3 + 1]
        row0 = jnp.minimum(row // 8, spec_ref.shape[1] - tiles - 1)
        col0 = jnp.minimum(col // window, spec_ref.shape[3] // window - 2)
        row_s = row - row0 * 8
        col_s = col - col0 * window
        lanes = pl.multiple_of(col0 * window, window)
        lanes2 = pl.multiple_of(col0 * window + window, window)
        sub8 = lax.broadcasted_iota(jnp.int32, (tiles, 8, window), 1)
        lane17 = lax.broadcasted_iota(jnp.int32, (tiles + 1, 8, window), 2)
        col_back = lax.rem(window - col_s, window)
        row_back = lax.rem(8 - row_s, 8)
        cut = []
        for plane in range(2):
            first = spec_ref[plane, pl.ds(row0, tiles + 1), :, pl.ds(lanes, window)]
            second = spec_ref[plane, pl.ds(row0, tiles + 1), :, pl.ds(lanes2, window)]
            joined = jnp.where(
                lane17 < window - col_s,
                pltpu.roll(first, col_back, 2),
                pltpu.roll(second, col_back, 2),
            )
            turned = pltpu.roll(joined, row_back, 1)
            picked = jnp.where(sub8 < 8 - row_s, turned[:tiles], turned[1:])
            cut.append(picked.reshape(window, window))
        w_re, w_im = cut
        grad_ref[modes * 2] += w_re * w_re + w_im * w_im

        power = jnp.zeros((window, window), jnp.float32)
        for pair in range(0, modes, 2):
            top, low = [], []
            for m in (pair, pair + 1):
                p_re, p_im = probe_ref[m, 0], probe_ref[m, 1]
                top.append(p_re * w_re - p_im * w_im)
                low.append(p_re * w_im + p_im * w_re)
            wave = jnp.concatenate(
                [jnp.concatenate(top, axis=1), jnp.concatenate(low, axis=1)], axis=0
            )
            mid = left(table_ref[0], table_ref[1], wave)
            for k, m in enumerate((pair, pair + 1)):
                lane = slice(k * window, (k + 1) * window)
                side = jnp.concatenate([mid[:window, lane], mid[window:, lane]], axis=1)
                far = right(side, table_ref[2], table_ref[3])
                far_ref[m] = far
                power = power + (far[:, :window] ** 2 + far[:, window:] ** 2)
        factor = jnp.sqrt(pattern_ref[0]) / jnp.maximum(jnp.sqrt(power), AMP_FLOOR) - 1.0
        factor2 = jnp.concatenate([factor, factor], axis=1)
        g_re = jnp.zeros((window, window), jnp.float32)
        g_im = jnp.zeros((window, window), jnp.float32)
        for pair in range(0, modes, 2):
            top, low = [], []
            for m in (pair, pair + 1):
                side = right(far_ref[m] * factor2, table_ref[0], table_ref[1])
                top.append(side[:, :window])
                low.append(side[:, window:])
            mid = jnp.concatenate(
                [jnp.concatenate(top, axis=1), jnp.concatenate(low, axis=1)], axis=0
            )
            back = left(table_ref[2], table_ref[3], mid)
            for k, m in enumerate((pair, pair + 1)):
                lane = slice(k * window, (k + 1) * window)
                b_re, b_im = back[:window, lane], back[window:, lane]
                p_re, p_im = probe_ref[m, 0], probe_ref[m, 1]
                g_re = g_re + (p_re * b_re + p_im * b_im)
                g_im = g_im + (p_re * b_im - p_im * b_re)
                grad_ref[2 * m] += w_re * b_re + w_im * b_im
                grad_ref[2 * m + 1] += w_re * b_im - w_im * b_re

        scale = scale_ref[0]
        lane16 = lax.broadcasted_iota(jnp.int32, (tiles + 1, 8, window), 2)
        sub17 = lax.broadcasted_iota(jnp.int32, (tiles + 1, 8, window), 1)
        row_turn = lax.rem(row_s, 8)
        col_turn = lax.rem(col_s, window)
        none = jnp.zeros((1, 8, window), jnp.float32)
        for plane, grad in enumerate((g_re, g_im)):
            turned = pltpu.roll((grad * scale).reshape(tiles, 8, window), row_turn, 1)
            spread = jnp.where(
                sub17 >= row_s,
                jnp.concatenate([turned, none], axis=0),
                jnp.concatenate([none, turned], axis=0),
            )
            spread = pltpu.roll(spread, col_turn, 2)
            out_ref[plane, pl.ds(row0, tiles + 1), :, pl.ds(lanes, window)] += jnp.where(
                lane16 >= col_s, spread, 0.0
            )
            out_ref[plane, pl.ds(row0, tiles + 1), :, pl.ds(lanes2, window)] += jnp.where(
                lane16 < col_s, spread, 0.0
            )


def sweep(requests, specimen, probe_modes, tables, measured):
    slots, window, _ = measured.shape
    modes = probe_modes.shape[0]
    whole = lambda shape: pl.BlockSpec(shape, lambda i: (0,) * len(shape))
    return pl.pallas_call(
        sweep_kernel,
        grid=(slots,),
        out_shape=(
            jax.ShapeDtypeStruct(specimen.shape, jnp.float32),
            jax.ShapeDtypeStruct((2 * modes + 1, window, window), jnp.float32),
        ),
        in_specs=[
            pl.BlockSpec(memory_space=SMEM),
            whole(specimen.shape),
            whole(probe_modes.shape),
            whole(tables.shape),
            pl.BlockSpec((1, window, window), lambda i: (i, 0, 0)),
        ],
        out_specs=(whole(specimen.shape), whole((2 * modes + 1, window, window))),
        scratch_shapes=[
            pltpu.SMEM((1,), jnp.float32),
            pltpu.VMEM((modes, window, 2 * window), jnp.float32),
        ],
        compiler_params=pltpu.CompilerParams(
            dimension_semantics=("arbitrary",), vmem_limit_bytes=LIMIT
        ),
        name="sweep",
    )(requests, specimen, probe_modes, tables, measured)


def shards(specimen, probe_modes, patterns, tile_row, row_offset, col_offset):
    own_count = patterns.shape[0]
    window = patterns.shape[-1]
    modes = probe_modes.shape[0]
    grid_rows = lax.axis_size("ty")
    capacity = max(2, 2 * own_count // grid_rows)
    slots = grid_rows * capacity
    tables = jnp.asarray(dft_tables(window))
    pattern_grid, requests = bucket(tile_row, row_offset, col_offset, patterns, slots, capacity)
    seen = lax.all_to_all(
        requests.reshape(grid_rows, capacity * 3), "ty", split_axis=0, concat_axis=0, tiled=True
    ).reshape(slots * 3)
    measured = lax.all_to_all(
        pattern_grid.reshape(grid_rows, capacity, window, window),
        "ty", split_axis=0, concat_axis=0, tiled=True,
    ).reshape(slots, window, window)
    shape = specimen.shape
    specimen = specimen.reshape(2, shape[1] // 8, 8, shape[2])
    for sweep_index in range(ITERS):
        specimen, grads = sweep(seen, specimen, probe_modes, tables, measured)
        total = lax.psum(grads, ("ty", "tx"))
        probe_modes = probe_modes + total[: 2 * modes].reshape(probe_modes.shape) / (
            jnp.max(total[2 * modes]) + SMALL_EPS
        )
    return (specimen.reshape(shape), probe_modes)


def solution(mesh):
    placed = (
        P(None, "ty", "tx"),
        P(),
        P(("ty", "tx"), None, None),
        P(("ty", "tx")),
        P(("ty", "tx")),
        P(("ty", "tx")),
    )
    return jax.shard_map(
        shards, mesh=mesh, in_specs=placed, out_specs=(P(None, "ty", "tx"), P()), check_vma=False
    )
```

```python
import functools
import math

import jax
import jax.numpy as jnp
import ml_dtypes
import numpy as np
from jax import lax
from jax.experimental import pallas as pl
from jax.experimental.pallas import tpu as pltpu
from jax.sharding import PartitionSpec as P

ITERS = 2
AMP_FLOOR = 0.3
OBJ_STEP = 1.0
SMALL_EPS = 1e-06

VMEM = pltpu.VMEM
SMEM = pltpu.SMEM
LIMIT = 50 * 1024 * 1024


def dft_tables(length):
    counter = np.arange(length, dtype=np.int64)
    angles = (counter[:, None] * counter[None, :] % length) * (2.0 * math.pi / length)
    cos = np.cos(angles) / math.sqrt(length)
    sin = np.sin(angles) / math.sqrt(length)
    one = np.block([[cos, sin], [-sin, cos]])
    parts = []
    for table in (one, one.T):
        high = table.astype(ml_dtypes.bfloat16)
        low = (table - high.astype(np.float64)).astype(ml_dtypes.bfloat16)
        parts += [high, low]
    return np.stack(parts)


def split(values):
    high = values.astype(jnp.bfloat16)
    low = (values - high.astype(jnp.float32)).astype(jnp.bfloat16)
    return high, low


def dot(a, b):
    return jnp.dot(a, b, preferred_element_type=jnp.float32)


def left(high, low, values):
    v_high, v_low = split(values)
    return dot(high, v_high) + (dot(low, v_high) + dot(high, v_low))


def right(values, high, low):
    v_high, v_low = split(values)
    return dot(v_high, high) + (dot(v_low, high) + dot(v_high, low))


def bucket_kernel(capacity, tile_ref, row_ref, col_ref, patterns_ref, grid_ref, req_ref):
    own, window, _ = patterns_ref.shape
    req_ref[...] = jnp.zeros_like(req_ref)
    for p in range(own):
        tile = tile_ref[p]
        rank = jnp.int32(0)
        for q in range(p):
            rank = rank + (tile_ref[q] == tile).astype(jnp.int32)
        grid_ref[tile * capacity + rank] = patterns_ref[p]
        for k, value in enumerate((row_ref[p], col_ref[p], jnp.int32(1))):
            req_ref[tile, pl.ds(rank * 3 + k, 1), :] = jnp.full((1, window), value, jnp.int32)


def bucket(tile_row, row_offset, col_offset, patterns, grid_rows, capacity):
    window = patterns.shape[-1]
    head = -(-capacity * 3 // 8) * 8
    return pl.pallas_call(
        functools.partial(bucket_kernel, capacity),
        out_shape=(
            jax.ShapeDtypeStruct((grid_rows * capacity, window, window), jnp.float32),
            jax.ShapeDtypeStruct((grid_rows, head, window), jnp.int32),
        ),
        in_specs=[pl.BlockSpec(memory_space=SMEM)] * 3 + [pl.BlockSpec(memory_space=VMEM)],
        out_specs=(pl.BlockSpec(memory_space=VMEM), pl.BlockSpec(memory_space=VMEM)),
        name="bucket",
    )(tile_row, row_offset, col_offset, patterns)


def far_first(count):
    return sorted(range(1, count), key=lambda d: -min(d, count - d))


def exchange_kernel(count, grid_ref, req_ref, got_ref, seen_ref, own_sem, send_sem, recv_sem, hsend, hrecv):
    me = lax.axis_index("ty")
    barrier = pltpu.get_barrier_semaphore()
    for d in range(1, count):
        pl.semaphore_signal(
            barrier, inc=1, device_id={"ty": lax.rem(me + d, count)}, device_id_type=pl.DeviceIdType.MESH
        )
    pl.semaphore_wait(barrier, count - 1)
    copies = []
    for d in range(1, count):
        peer = lax.rem(me + d, count)
        copies.append(pltpu.make_async_remote_copy(
            src_ref=req_ref.at[peer], dst_ref=seen_ref.at[me],
            send_sem=hsend.at[d - 1], recv_sem=hrecv.at[d - 1],
            device_id={"ty": peer}, device_id_type=pl.DeviceIdType.MESH,
        ))
        copies[-1].start()
    for d in far_first(count):
        peer = lax.rem(me + d, count)
        copies.append(pltpu.make_async_remote_copy(
            src_ref=grid_ref.at[peer], dst_ref=got_ref.at[me],
            send_sem=send_sem.at[d - 1], recv_sem=recv_sem.at[d - 1],
            device_id={"ty": peer}, device_id_type=pl.DeviceIdType.MESH,
        ))
        copies[-1].start()
    own = [
        pltpu.make_async_copy(grid_ref.at[me], got_ref.at[me], own_sem.at[0]),
        pltpu.make_async_copy(req_ref.at[me], seen_ref.at[me], own_sem.at[1]),
    ]
    for copy in own:
        copy.start()
    for copy in own + copies:
        copy.wait()


def exchange(grid, requests):
    count = grid.shape[0]
    dma = pltpu.SemaphoreType.DMA
    return pl.pallas_call(
        functools.partial(exchange_kernel, count),
        out_shape=(
            jax.ShapeDtypeStruct(grid.shape, grid.dtype),
            jax.ShapeDtypeStruct(requests.shape, requests.dtype),
        ),
        in_specs=[pl.BlockSpec(memory_space=VMEM)] * 2,
        out_specs=(pl.BlockSpec(memory_space=pl.ANY),) * 2,
        scratch_shapes=[dma((2,))] + [dma((count - 1,))] * 4,
        compiler_params=pltpu.CompilerParams(collective_id=0, has_side_effects=True),
        name="exchange",
    )(grid, requests)


def total_kernel(ny, nty, g_ref, out_ref, half, part, piece, in_y, in_ty, full, *sems):
    core_s, core_r, y_s, y_r, ty_s, ty_r, ty_s2, ty_r2, y_s2, y_r2, core_s2, core_r2 = sems
    ty, tx = lax.axis_index("ty"), lax.axis_index("tx")
    core, y = lax.rem(tx, 2), tx // 2
    mate = {"tx": y * 2 + 1 - core}
    y_ids = [lax.rem(y + d, ny) for d in range(1, ny)]
    ty_ids = [lax.rem(ty + d, nty) for d in range(1, nty)]
    y_dev = [{"tx": peer * 2 + core} for peer in y_ids]
    ty_dev = [{"ty": peer} for peer in ty_ids]
    mesh_id = pl.DeviceIdType.MESH
    barrier = pltpu.get_barrier_semaphore()
    for device in [mate] + y_dev + ty_dev:
        pl.semaphore_signal(barrier, inc=1, device_id=device, device_id_type=mesh_id)
    pl.semaphore_wait(barrier, 1 + len(y_dev) + len(ty_dev))

    def send(src, dst, s, r, device):
        copy = pltpu.make_async_remote_copy(
            src_ref=src, dst_ref=dst, send_sem=s, recv_sem=r, device_id=device, device_id_type=mesh_id
        )
        copy.start()
        return copy

    send(g_ref.at[1 - core], half, core_s.at[0], core_r.at[0], mate).wait()
    part[...] = g_ref[core] + half[...]
    copies = [
        send(part.at[y_ids[d]], in_y.at[d], y_s.at[d], y_r.at[d], y_dev[d]) for d in range(ny - 1)
    ]
    acc = part[y]
    for d, copy in enumerate(copies):
        copy.wait()
        acc = acc + in_y[d]
    piece[...] = acc
    order = [d - 1 for d in far_first(nty)]
    copies = {
        d: send(piece.at[ty_ids[d]], in_ty.at[d], ty_s.at[d], ty_r.at[d], ty_dev[d]) for d in order
    }
    acc = piece[ty]
    for d in range(nty - 1):
        copies[d].wait()
        acc = acc + in_ty[d]
    full[core, y, ty] = acc
    mine = full.at[core, y, ty]
    copies = [send(mine, mine, ty_s2.at[d], ty_r2.at[d], ty_dev[d]) for d in order]
    for copy in copies:
        copy.wait()
    mine = full.at[core, y]
    copies = [send(mine, mine, y_s2.at[d], y_r2.at[d], y_dev[d]) for d in range(ny - 1)]
    for copy in copies:
        copy.wait()
    mine = full.at[core]
    send(mine, mine, core_s2.at[0], core_r2.at[0], mate).wait()
    out_ref[...] = full[...]


def total_over_devices(grads):
    window = grads.shape[-1]
    nty, ny = lax.axis_size("ty"), lax.axis_size("tx") // 2
    c = grads.size // (2 * ny * nty * 8 * window)
    shape = (2, ny, nty, c, 8, window)
    f32 = jnp.float32
    dma = pltpu.SemaphoreType.DMA
    y_n, ty_n = max(ny - 1, 1), max(nty - 1, 1)
    total = pl.pallas_call(
        functools.partial(total_kernel, ny, nty),
        out_shape=jax.ShapeDtypeStruct(shape, f32),
        in_specs=[pl.BlockSpec(memory_space=VMEM)],
        out_specs=pl.BlockSpec(memory_space=VMEM),
        scratch_shapes=[
            VMEM(shape[1:], f32),
            VMEM(shape[1:], f32),
            VMEM(shape[2:], f32),
            VMEM((y_n,) + shape[2:], f32),
            VMEM((ty_n,) + shape[3:], f32),
            VMEM(shape, f32),
        ] + [dma((n,)) for n in (1, 1, y_n, y_n, ty_n, ty_n, ty_n, ty_n, y_n, y_n, 1, 1)],
        compiler_params=pltpu.CompilerParams(collective_id=1, has_side_effects=True),
        name="total",
    )(grads.reshape(shape))
    return total.reshape(grads.shape)


def update_kernel(total_ref, probe_ref, out_ref):
    planes = probe_ref.shape[0]
    bottom = jnp.max(total_ref[planes]) + SMALL_EPS
    out_ref[...] = probe_ref[...] + total_ref[:planes] / bottom


def update(total, probe_modes):
    modes, _, window, _ = probe_modes.shape
    shape = (2 * modes, window, window)
    return pl.pallas_call(
        update_kernel,
        out_shape=jax.ShapeDtypeStruct(shape, jnp.float32),
        in_specs=[pl.BlockSpec(memory_space=VMEM)] * 2,
        out_specs=pl.BlockSpec(memory_space=VMEM),
        name="update",
    )(total, probe_modes.reshape(shape)).reshape(probe_modes.shape)


def sweep_kernel(req_ref, spec_ref, probe_ref, table_ref, pattern_ref, out_ref, grad_ref, scale_ref, far_ref):
    step = pl.program_id(0)
    modes, _, window, _ = probe_ref.shape
    tiles = window // 8

    @pl.when(step == 0)
    def _():
        out_ref[...] = spec_ref[...]
        grad_ref[...] = jnp.zeros_like(grad_ref)
        power = jnp.zeros((window, window), jnp.float32)
        for m in range(modes):
            power = power + (probe_ref[m, 0] ** 2 + probe_ref[m, 1] ** 2)
        scale_ref[0] = OBJ_STEP / (jnp.max(power) + SMALL_EPS)

    @pl.when(req_ref[step * 3 + 2] > 0)
    def _():
        row = req_ref[step * 3]
        col = req_ref[step * 3 + 1]
        row0 = jnp.minimum(row // 8, spec_ref.shape[1] - tiles - 1)
        col0 = jnp.minimum(col // window, spec_ref.shape[3] // window - 2)
        row_s = row - row0 * 8
        col_s = col - col0 * window
        lanes = pl.multiple_of(col0 * window, window)
        lanes2 = pl.multiple_of(col0 * window + window, window)
        sub8 = lax.broadcasted_iota(jnp.int32, (tiles, 8, window), 1)
        lane17 = lax.broadcasted_iota(jnp.int32, (tiles + 1, 8, window), 2)
        col_back = lax.rem(window - col_s, window)
        row_back = lax.rem(8 - row_s, 8)
        cut = []
        for plane in range(2):
            first = spec_ref[plane, pl.ds(row0, tiles + 1), :, pl.ds(lanes, window)]
            second = spec_ref[plane, pl.ds(row0, tiles + 1), :, pl.ds(lanes2, window)]
            joined = jnp.where(
                lane17 < window - col_s,
                pltpu.roll(first, col_back, 2),
                pltpu.roll(second, col_back, 2),
            )
            turned = pltpu.roll(joined, row_back, 1)
            picked = jnp.where(sub8 < 8 - row_s, turned[:tiles], turned[1:])
            cut.append(picked.reshape(window, window))
        w_re, w_im = cut
        grad_ref[modes * 2] += w_re * w_re + w_im * w_im

        power = jnp.zeros((window, window), jnp.float32)
        for pair in range(0, modes, 2):
            top, low = [], []
            for m in (pair, pair + 1):
                p_re, p_im = probe_ref[m, 0], probe_ref[m, 1]
                top.append(p_re * w_re - p_im * w_im)
                low.append(p_re * w_im + p_im * w_re)
            wave = jnp.concatenate(
                [jnp.concatenate(top, axis=1), jnp.concatenate(low, axis=1)], axis=0
            )
            mid = left(table_ref[0], table_ref[1], wave)
            for k, m in enumerate((pair, pair + 1)):
                lane = slice(k * window, (k + 1) * window)
                side = jnp.concatenate([mid[:window, lane], mid[window:, lane]], axis=1)
                far = right(side, table_ref[2], table_ref[3])
                far_ref[m] = far
                power = power + (far[:, :window] ** 2 + far[:, window:] ** 2)
        factor = jnp.sqrt(pattern_ref[0]) / jnp.maximum(jnp.sqrt(power), AMP_FLOOR) - 1.0
        factor2 = jnp.concatenate([factor, factor], axis=1)
        g_re = jnp.zeros((window, window), jnp.float32)
        g_im = jnp.zeros((window, window), jnp.float32)
        for pair in range(0, modes, 2):
            top, low = [], []
            for m in (pair, pair + 1):
                side = right(far_ref[m] * factor2, table_ref[0], table_ref[1])
                top.append(side[:, :window])
                low.append(side[:, window:])
            mid = jnp.concatenate(
                [jnp.concatenate(top, axis=1), jnp.concatenate(low, axis=1)], axis=0
            )
            back = left(table_ref[2], table_ref[3], mid)
            for k, m in enumerate((pair, pair + 1)):
                lane = slice(k * window, (k + 1) * window)
                b_re, b_im = back[:window, lane], back[window:, lane]
                p_re, p_im = probe_ref[m, 0], probe_ref[m, 1]
                g_re = g_re + (p_re * b_re + p_im * b_im)
                g_im = g_im + (p_re * b_im - p_im * b_re)
                grad_ref[2 * m] += w_re * b_re + w_im * b_im
                grad_ref[2 * m + 1] += w_re * b_im - w_im * b_re

        scale = scale_ref[0]
        lane16 = lax.broadcasted_iota(jnp.int32, (tiles + 1, 8, window), 2)
        sub17 = lax.broadcasted_iota(jnp.int32, (tiles + 1, 8, window), 1)
        row_turn = lax.rem(row_s, 8)
        col_turn = lax.rem(col_s, window)
        none = jnp.zeros((1, 8, window), jnp.float32)
        for plane, grad in enumerate((g_re, g_im)):
            turned = pltpu.roll((grad * scale).reshape(tiles, 8, window), row_turn, 1)
            spread = jnp.where(
                sub17 >= row_s,
                jnp.concatenate([turned, none], axis=0),
                jnp.concatenate([none, turned], axis=0),
            )
            spread = pltpu.roll(spread, col_turn, 2)
            out_ref[plane, pl.ds(row0, tiles + 1), :, pl.ds(lanes, window)] += jnp.where(
                lane16 >= col_s, spread, 0.0
            )
            out_ref[plane, pl.ds(row0, tiles + 1), :, pl.ds(lanes2, window)] += jnp.where(
                lane16 < col_s, spread, 0.0
            )


def sweep(requests, specimen, probe_modes, tables, measured, blocks):
    slots, window, _ = measured.shape
    modes = probe_modes.shape[0]
    whole = lambda shape: pl.BlockSpec(shape, lambda i: (0,) * len(shape))
    return pl.pallas_call(
        sweep_kernel,
        grid=(slots,),
        out_shape=(
            jax.ShapeDtypeStruct(specimen.shape, jnp.float32),
            jax.ShapeDtypeStruct((blocks, window, window), jnp.float32),
        ),
        in_specs=[
            pl.BlockSpec(memory_space=SMEM),
            whole(specimen.shape),
            whole(probe_modes.shape),
            whole(tables.shape),
            pl.BlockSpec((1, window, window), lambda i: (i, 0, 0)),
        ],
        out_specs=(whole(specimen.shape), whole((blocks, window, window))),
        scratch_shapes=[
            pltpu.SMEM((1,), jnp.float32),
            pltpu.VMEM((modes, window, 2 * window), jnp.float32),
        ],
        compiler_params=pltpu.CompilerParams(
            dimension_semantics=("arbitrary",), vmem_limit_bytes=LIMIT
        ),
        name="sweep",
    )(requests, specimen, probe_modes, tables, measured)


def shards(specimen, probe_modes, patterns, tile_row, row_offset, col_offset):
    own_count = patterns.shape[0]
    window = patterns.shape[-1]
    modes = probe_modes.shape[0]
    grid_rows = lax.axis_size("ty")
    capacity = max(2, 2 * own_count // grid_rows)
    slots = grid_rows * capacity
    tables = jnp.asarray(dft_tables(window))
    pattern_grid, requests = bucket(tile_row, row_offset, col_offset, patterns, grid_rows, capacity)
    measured, seen = exchange(
        pattern_grid.reshape(grid_rows, capacity, window, window), requests
    )
    measured = measured.reshape(slots, window, window)
    seen = seen[:, : capacity * 3, 0].reshape(slots * 3)
    devices = grid_rows * lax.axis_size("tx")
    tiles = window // 8
    per_device = -(-(2 * modes + 1) * tiles // devices)
    blocks = -(-per_device * devices // tiles)
    shape = specimen.shape
    specimen = specimen.reshape(2, shape[1] // 8, 8, shape[2])
    for sweep_index in range(ITERS):
        specimen, grads = sweep(seen, specimen, probe_modes, tables, measured, blocks)
        probe_modes = update(total_over_devices(grads), probe_modes)
    return (specimen.reshape(shape), probe_modes)


def solution(mesh):
    placed = (
        P(None, "ty", "tx"),
        P(),
        P(("ty", "tx"), None, None),
        P(("ty", "tx")),
        P(("ty", "tx")),
        P(("ty", "tx")),
    )
    return jax.shard_map(
        shards, mesh=mesh, in_specs=placed, out_specs=(P(None, "ty", "tx"), P()), check_vma=False
    )
```

```python
import functools
import math

import jax
import jax.numpy as jnp
import ml_dtypes
import numpy as np
from jax import lax
from jax.experimental import pallas as pl
from jax.experimental.pallas import tpu as pltpu
from jax.sharding import PartitionSpec as P

ITERS = 2
AMP_FLOOR = 0.3
OBJ_STEP = 1.0
SMALL_EPS = 1e-06

VMEM = pltpu.VMEM
SMEM = pltpu.SMEM
LIMIT = 50 * 1024 * 1024


def dft_tables(length):
    counter = np.arange(length, dtype=np.int64)
    angles = (counter[:, None] * counter[None, :] % length) * (2.0 * math.pi / length)
    cos = np.cos(angles) / math.sqrt(length)
    sin = np.sin(angles) / math.sqrt(length)
    one = np.block([[cos, sin], [-sin, cos]])
    parts = []
    for table in (one, one.T):
        high = table.astype(ml_dtypes.bfloat16)
        low = (table - high.astype(np.float64)).astype(ml_dtypes.bfloat16)
        parts += [high, low]
    return np.stack(parts)


def split(values):
    high = values.astype(jnp.bfloat16)
    low = (values - high.astype(jnp.float32)).astype(jnp.bfloat16)
    return high, low


def dot(a, b):
    return jnp.dot(a, b, preferred_element_type=jnp.float32)


def left(high, low, values):
    v_high, v_low = split(values)
    return dot(high, v_high) + (dot(low, v_high) + dot(high, v_low))


def right(values, high, low):
    v_high, v_low = split(values)
    return dot(v_high, high) + (dot(v_low, high) + dot(v_high, low))


def bucket_kernel(capacity, tile_ref, row_ref, col_ref, patterns_ref, grid_ref, req_ref):
    own, window, _ = patterns_ref.shape
    req_ref[...] = jnp.zeros_like(req_ref)
    for p in range(own):
        tile = tile_ref[p]
        rank = jnp.int32(0)
        for q in range(p):
            rank = rank + (tile_ref[q] == tile).astype(jnp.int32)
        grid_ref[tile * capacity + rank] = patterns_ref[p]
        for k, value in enumerate((row_ref[p], col_ref[p], jnp.int32(1))):
            req_ref[tile, pl.ds(rank * 3 + k, 1), :] = jnp.full((1, window), value, jnp.int32)


def bucket(tile_row, row_offset, col_offset, patterns, grid_rows, capacity):
    window = patterns.shape[-1]
    head = -(-capacity * 3 // 8) * 8
    return pl.pallas_call(
        functools.partial(bucket_kernel, capacity),
        out_shape=(
            jax.ShapeDtypeStruct((grid_rows * capacity, window, window), jnp.float32),
            jax.ShapeDtypeStruct((grid_rows, head, window), jnp.int32),
        ),
        in_specs=[pl.BlockSpec(memory_space=SMEM)] * 3 + [pl.BlockSpec(memory_space=VMEM)],
        out_specs=(pl.BlockSpec(memory_space=VMEM), pl.BlockSpec(memory_space=VMEM)),
        name="bucket",
    )(tile_row, row_offset, col_offset, patterns)


def far_first(count):
    return sorted(range(1, count), key=lambda d: -min(d, count - d))


def exchange_kernel(count, grid_ref, req_ref, got_ref, seen_ref, own_sem, send_sem, recv_sem, hsend, hrecv):
    me = lax.axis_index("ty")
    barrier = pltpu.get_barrier_semaphore()
    for d in range(1, count):
        pl.semaphore_signal(
            barrier, inc=1, device_id={"ty": lax.rem(me + d, count)}, device_id_type=pl.DeviceIdType.MESH
        )
    pl.semaphore_wait(barrier, count - 1)
    copies = []
    for d in range(1, count):
        peer = lax.rem(me + d, count)
        copies.append(pltpu.make_async_remote_copy(
            src_ref=req_ref.at[peer], dst_ref=seen_ref.at[me],
            send_sem=hsend.at[d - 1], recv_sem=hrecv.at[d - 1],
            device_id={"ty": peer}, device_id_type=pl.DeviceIdType.MESH,
        ))
        copies[-1].start()
    for d in far_first(count):
        peer = lax.rem(me + d, count)
        copies.append(pltpu.make_async_remote_copy(
            src_ref=grid_ref.at[peer], dst_ref=got_ref.at[me],
            send_sem=send_sem.at[d - 1], recv_sem=recv_sem.at[d - 1],
            device_id={"ty": peer}, device_id_type=pl.DeviceIdType.MESH,
        ))
        copies[-1].start()
    own = [
        pltpu.make_async_copy(grid_ref.at[me], got_ref.at[me], own_sem.at[0]),
        pltpu.make_async_copy(req_ref.at[me], seen_ref.at[me], own_sem.at[1]),
    ]
    for copy in own:
        copy.start()
    for copy in own + copies:
        copy.wait()


def exchange(grid, requests):
    count = grid.shape[0]
    dma = pltpu.SemaphoreType.DMA
    return pl.pallas_call(
        functools.partial(exchange_kernel, count),
        out_shape=(
            jax.ShapeDtypeStruct(grid.shape, grid.dtype),
            jax.ShapeDtypeStruct(requests.shape, requests.dtype),
        ),
        in_specs=[pl.BlockSpec(memory_space=VMEM)] * 2,
        out_specs=(pl.BlockSpec(memory_space=pl.ANY),) * 2,
        scratch_shapes=[dma((2,))] + [dma((count - 1,))] * 4,
        compiler_params=pltpu.CompilerParams(collective_id=0, has_side_effects=True),
        name="exchange",
    )(grid, requests)


def total_kernel(ny, nty, g_ref, out_ref, half, part, piece, in_y, in_ty, full, *sems):
    core_s, core_r, y_s, y_r, ty_s, ty_r, ty_s2, ty_r2, y_s2, y_r2, core_s2, core_r2 = sems
    ty, tx = lax.axis_index("ty"), lax.axis_index("tx")
    core, y = lax.rem(tx, 2), tx // 2
    mate = {"tx": y * 2 + 1 - core}
    y_ids = [lax.rem(y + d, ny) for d in range(1, ny)]
    ty_ids = [lax.rem(ty + d, nty) for d in range(1, nty)]
    y_dev = [{"tx": peer * 2 + core} for peer in y_ids]
    ty_dev = [{"ty": peer} for peer in ty_ids]
    mesh_id = pl.DeviceIdType.MESH
    barrier = pltpu.get_barrier_semaphore()
    for device in [mate] + y_dev + ty_dev:
        pl.semaphore_signal(barrier, inc=1, device_id=device, device_id_type=mesh_id)
    pl.semaphore_wait(barrier, 1 + len(y_dev) + len(ty_dev))

    def send(src, dst, s, r, device):
        copy = pltpu.make_async_remote_copy(
            src_ref=src, dst_ref=dst, send_sem=s, recv_sem=r, device_id=device, device_id_type=mesh_id
        )
        copy.start()
        return copy

    halves = [
        send(g_ref.at[1 - core, k], half.at[k], core_s.at[d], core_r.at[d], mate)
        for d, k in enumerate(y_ids + [y])
    ]
    copies = []
    for d, k in enumerate(y_ids + [y]):
        halves[d].wait()
        part[k] = g_ref[core, k] + half[k]
        if d < ny - 1:
            copies.append(send(part.at[k], in_y.at[d], y_s.at[d], y_r.at[d], y_dev[d]))
    acc = part[y]
    for d, copy in enumerate(copies):
        copy.wait()
        acc = acc + in_y[d]
    piece[...] = acc
    order = [d - 1 for d in far_first(nty)]
    copies = {
        d: send(piece.at[ty_ids[d]], in_ty.at[d], ty_s.at[d], ty_r.at[d], ty_dev[d]) for d in order
    }
    acc = piece[ty]
    for d in range(nty - 1):
        copies[d].wait()
        acc = acc + in_ty[d]
    full[core, y, ty] = acc
    mine = full.at[core, y, ty]
    copies = [send(mine, mine, ty_s2.at[d], ty_r2.at[d], ty_dev[d]) for d in order]
    for copy in copies:
        copy.wait()
    mine = full.at[core, y]
    copies = [send(mine, mine, y_s2.at[d], y_r2.at[d], y_dev[d]) for d in range(ny - 1)]
    last = [send(mine, mine, core_s2.at[ny - 1], core_r2.at[ny - 1], mate)]
    for d, copy in enumerate(copies):
        copy.wait()
        other = full.at[core, lax.rem(y + ny - 1 - d, ny)]
        last.append(send(other, other, core_s2.at[d], core_r2.at[d], mate))
    for copy in last:
        copy.wait()
    out_ref[...] = full[...]


def total_over_devices(grads):
    window = grads.shape[-1]
    nty, ny = lax.axis_size("ty"), lax.axis_size("tx") // 2
    c = grads.size // (2 * ny * nty * 8 * window)
    shape = (2, ny, nty, c, 8, window)
    f32 = jnp.float32
    dma = pltpu.SemaphoreType.DMA
    y_n, ty_n = max(ny - 1, 1), max(nty - 1, 1)
    total = pl.pallas_call(
        functools.partial(total_kernel, ny, nty),
        out_shape=jax.ShapeDtypeStruct(shape, f32),
        in_specs=[pl.BlockSpec(memory_space=VMEM)],
        out_specs=pl.BlockSpec(memory_space=VMEM),
        scratch_shapes=[
            VMEM(shape[1:], f32),
            VMEM(shape[1:], f32),
            VMEM(shape[2:], f32),
            VMEM((y_n,) + shape[2:], f32),
            VMEM((ty_n,) + shape[3:], f32),
            VMEM(shape, f32),
        ] + [dma((n,)) for n in (ny, ny, y_n, y_n, ty_n, ty_n, ty_n, ty_n, y_n, y_n, ny, ny)],
        compiler_params=pltpu.CompilerParams(collective_id=1, has_side_effects=True),
        name="total",
    )(grads.reshape(shape))
    return total.reshape(grads.shape)


def update_kernel(total_ref, probe_ref, out_ref):
    planes = probe_ref.shape[0]
    bottom = jnp.max(total_ref[planes]) + SMALL_EPS
    out_ref[...] = probe_ref[...] + total_ref[:planes] / bottom


def update(total, probe_modes):
    modes, _, window, _ = probe_modes.shape
    shape = (2 * modes, window, window)
    return pl.pallas_call(
        update_kernel,
        out_shape=jax.ShapeDtypeStruct(shape, jnp.float32),
        in_specs=[pl.BlockSpec(memory_space=VMEM)] * 2,
        out_specs=pl.BlockSpec(memory_space=VMEM),
        name="update",
    )(total, probe_modes.reshape(shape)).reshape(probe_modes.shape)


def sweep_kernel(req_ref, spec_ref, probe_ref, table_ref, pattern_ref, out_ref, grad_ref, scale_ref, far_ref):
    step = pl.program_id(0)
    modes, _, window, _ = probe_ref.shape
    tiles = window // 8

    @pl.when(step == 0)
    def _():
        out_ref[...] = spec_ref[...]
        grad_ref[...] = jnp.zeros_like(grad_ref)
        power = jnp.zeros((window, window), jnp.float32)
        for m in range(modes):
            power = power + (probe_ref[m, 0] ** 2 + probe_ref[m, 1] ** 2)
        scale_ref[0] = OBJ_STEP / (jnp.max(power) + SMALL_EPS)

    @pl.when(req_ref[step * 3 + 2] > 0)
    def _():
        row = req_ref[step * 3]
        col = req_ref[step * 3 + 1]
        row0 = jnp.minimum(row // 8, spec_ref.shape[1] - tiles - 1)
        col0 = jnp.minimum(col // window, spec_ref.shape[3] // window - 2)
        row_s = row - row0 * 8
        col_s = col - col0 * window
        lanes = pl.multiple_of(col0 * window, window)
        lanes2 = pl.multiple_of(col0 * window + window, window)
        sub8 = lax.broadcasted_iota(jnp.int32, (tiles, 8, window), 1)
        lane17 = lax.broadcasted_iota(jnp.int32, (tiles + 1, 8, window), 2)
        col_back = lax.rem(window - col_s, window)
        row_back = lax.rem(8 - row_s, 8)
        cut = []
        for plane in range(2):
            first = spec_ref[plane, pl.ds(row0, tiles + 1), :, pl.ds(lanes, window)]
            second = spec_ref[plane, pl.ds(row0, tiles + 1), :, pl.ds(lanes2, window)]
            joined = jnp.where(
                lane17 < window - col_s,
                pltpu.roll(first, col_back, 2),
                pltpu.roll(second, col_back, 2),
            )
            turned = pltpu.roll(joined, row_back, 1)
            picked = jnp.where(sub8 < 8 - row_s, turned[:tiles], turned[1:])
            cut.append(picked.reshape(window, window))
        w_re, w_im = cut
        grad_ref[modes * 2] += w_re * w_re + w_im * w_im

        power = jnp.zeros((window, window), jnp.float32)
        for pair in range(0, modes, 2):
            top, low = [], []
            for m in (pair, pair + 1):
                p_re, p_im = probe_ref[m, 0], probe_ref[m, 1]
                top.append(p_re * w_re - p_im * w_im)
                low.append(p_re * w_im + p_im * w_re)
            wave = jnp.concatenate(
                [jnp.concatenate(top, axis=1), jnp.concatenate(low, axis=1)], axis=0
            )
            mid = left(table_ref[0], table_ref[1], wave)
            for k, m in enumerate((pair, pair + 1)):
                lane = slice(k * window, (k + 1) * window)
                side = jnp.concatenate([mid[:window, lane], mid[window:, lane]], axis=1)
                far = right(side, table_ref[2], table_ref[3])
                far_ref[m] = far
                power = power + (far[:, :window] ** 2 + far[:, window:] ** 2)
        factor = jnp.sqrt(pattern_ref[0]) / jnp.maximum(jnp.sqrt(power), AMP_FLOOR) - 1.0
        factor2 = jnp.concatenate([factor, factor], axis=1)
        g_re = jnp.zeros((window, window), jnp.float32)
        g_im = jnp.zeros((window, window), jnp.float32)
        for pair in range(0, modes, 2):
            top, low = [], []
            for m in (pair, pair + 1):
                side = right(far_ref[m] * factor2, table_ref[0], table_ref[1])
                top.append(side[:, :window])
                low.append(side[:, window:])
            mid = jnp.concatenate(
                [jnp.concatenate(top, axis=1), jnp.concatenate(low, axis=1)], axis=0
            )
            back = left(table_ref[2], table_ref[3], mid)
            for k, m in enumerate((pair, pair + 1)):
                lane = slice(k * window, (k + 1) * window)
                b_re, b_im = back[:window, lane], back[window:, lane]
                p_re, p_im = probe_ref[m, 0], probe_ref[m, 1]
                g_re = g_re + (p_re * b_re + p_im * b_im)
                g_im = g_im + (p_re * b_im - p_im * b_re)
                grad_ref[2 * m] += w_re * b_re + w_im * b_im
                grad_ref[2 * m + 1] += w_re * b_im - w_im * b_re

        scale = scale_ref[0]
        lane16 = lax.broadcasted_iota(jnp.int32, (tiles + 1, 8, window), 2)
        sub17 = lax.broadcasted_iota(jnp.int32, (tiles + 1, 8, window), 1)
        row_turn = lax.rem(row_s, 8)
        col_turn = lax.rem(col_s, window)
        none = jnp.zeros((1, 8, window), jnp.float32)
        for plane, grad in enumerate((g_re, g_im)):
            turned = pltpu.roll((grad * scale).reshape(tiles, 8, window), row_turn, 1)
            spread = jnp.where(
                sub17 >= row_s,
                jnp.concatenate([turned, none], axis=0),
                jnp.concatenate([none, turned], axis=0),
            )
            spread = pltpu.roll(spread, col_turn, 2)
            out_ref[plane, pl.ds(row0, tiles + 1), :, pl.ds(lanes, window)] += jnp.where(
                lane16 >= col_s, spread, 0.0
            )
            out_ref[plane, pl.ds(row0, tiles + 1), :, pl.ds(lanes2, window)] += jnp.where(
                lane16 < col_s, spread, 0.0
            )


def sweep(requests, specimen, probe_modes, tables, measured, blocks):
    slots, window, _ = measured.shape
    modes = probe_modes.shape[0]
    whole = lambda shape: pl.BlockSpec(shape, lambda i: (0,) * len(shape))
    return pl.pallas_call(
        sweep_kernel,
        grid=(slots,),
        out_shape=(
            jax.ShapeDtypeStruct(specimen.shape, jnp.float32),
            jax.ShapeDtypeStruct((blocks, window, window), jnp.float32),
        ),
        in_specs=[
            pl.BlockSpec(memory_space=SMEM),
            whole(specimen.shape),
            whole(probe_modes.shape),
            whole(tables.shape),
            pl.BlockSpec((1, window, window), lambda i: (i, 0, 0)),
        ],
        out_specs=(whole(specimen.shape), whole((blocks, window, window))),
        scratch_shapes=[
            pltpu.SMEM((1,), jnp.float32),
            pltpu.VMEM((modes, window, 2 * window), jnp.float32),
        ],
        compiler_params=pltpu.CompilerParams(
            dimension_semantics=("arbitrary",), vmem_limit_bytes=LIMIT
        ),
        name="sweep",
    )(requests, specimen, probe_modes, tables, measured)


def shards(specimen, probe_modes, patterns, tile_row, row_offset, col_offset):
    own_count = patterns.shape[0]
    window = patterns.shape[-1]
    modes = probe_modes.shape[0]
    grid_rows = lax.axis_size("ty")
    capacity = max(2, 2 * own_count // grid_rows)
    slots = grid_rows * capacity
    tables = jnp.asarray(dft_tables(window))
    pattern_grid, requests = bucket(tile_row, row_offset, col_offset, patterns, grid_rows, capacity)
    measured, seen = exchange(
        pattern_grid.reshape(grid_rows, capacity, window, window), requests
    )
    measured = measured.reshape(slots, window, window)
    seen = seen[:, : capacity * 3, 0].reshape(slots * 3)
    devices = grid_rows * lax.axis_size("tx")
    tiles = window // 8
    per_device = -(-(2 * modes + 1) * tiles // devices)
    blocks = -(-per_device * devices // tiles)
    shape = specimen.shape
    specimen = specimen.reshape(2, shape[1] // 8, 8, shape[2])
    for sweep_index in range(ITERS):
        specimen, grads = sweep(seen, specimen, probe_modes, tables, measured, blocks)
        probe_modes = update(total_over_devices(grads), probe_modes)
    return (specimen.reshape(shape), probe_modes)


def solution(mesh):
    placed = (
        P(None, "ty", "tx"),
        P(),
        P(("ty", "tx"), None, None),
        P(("ty", "tx")),
        P(("ty", "tx")),
        P(("ty", "tx")),
    )
    return jax.shard_map(
        shards, mesh=mesh, in_specs=placed, out_specs=(P(None, "ty", "tx"), P()), check_vma=False
    )
```
